32 devices in a mesh: inner: 8 (over y, x, core), rows: 4 (over z).
Axes of the slice: x: 2, y: 2, z: 4, core: 2. Of those that a mesh axis runs over, the one named last changes fastest.
Arguments:
- left_u: bfloat16 [4, 32, 2048, 128], P('rows', 'inner'), may hold values from -6 to 6
- left_v: bfloat16 [4, 32, 2048, 128], P('rows', 'inner'), may hold values from -0.035888672 to 0.035888672
- tile_p: bfloat16 [4, 8, 2048, 128], P('rows'), may hold values from -6 to 6
- tile_q: bfloat16 [4, 8, 2048, 128], P('rows'), may hold values from -0.5390625 to 0.5390625
- sketch: bfloat16 [2048, 128], replicated, may hold values from -6 to 6
- tile_cols: int32 [4, 8], P('rows'), may hold values from 0 to 3
Outputs:
- new_left: float32 [4, 8, 2048, 128], P('rows', None, 'inner')
- new_right: float32 [4, 8, 2048, 128], P('rows', None, 'inner')
The draws below stay inside these ranges and needn't reach their ends.
All inputs are finite; a program needn't handle non-finite values.
Results may differ from the reference program's by a relative error of at most 0.0023.
Values may be sent and summed in bfloat16 or wider, within the bound.
No kernel may reach another device: no remote copies, remote signals or barrier semaphores. Data moves between devices by JAX's collectives and lax.ppermute only.
A program may use at most 128 MiB of HBM per device.

```python
import math
import jax
import jax.numpy as jnp
from jax import lax

B = 2048
R = 128
C = 8
NT = 4
K = 32


def set_ends(values, stream_key, least, top_value):
    index_at = [jax.random.randint(jax.random.fold_in(stream_key, axis), (), 0, length) for axis, length in enumerate(values.shape)]
    longest = values.shape.index(max(values.shape))
    next_to = index_at[:longest] + [(index_at[longest] + 1) % values.shape[longest]] + index_at[longest + 1:]
    return values.at[tuple(index_at)].set(least).at[tuple(next_to)].set(top_value)


def shard_levels(stream_key, dims, split, smallest, high):
    level = 1.0
    for position, shards_of in split:
        draws = jax.random.uniform(jax.random.fold_in(jax.random.fold_in(stream_key, 6), position), (shards_of,), jnp.float32, smallest / len(split), high / len(split))
        level = level * jnp.repeat(jnp.exp(draws), dims[position] // shards_of).reshape((-1,) + (1,) * (len(dims) - 1 - position))
    return level


def noise(stream_key, shape, deviation, reach, cuts=(), held_as=jnp.bfloat16):
    factor_of = shard_levels(stream_key, shape, cuts, -0.22, 0.18) if cuts else 1.0
    entries = jax.random.normal(stream_key, shape, jnp.float32) * deviation * factor_of
    return jnp.minimum(jnp.maximum(entries, -reach), reach).astype(held_as)


def setup_inputs(seed: int = 0) -> dict:
    arg_keys = jax.random.split(jax.random.key(seed), 7)
    return {
        "left_u": noise(arg_keys[0], (NT, K, B, R), 1.0, 6.0, ((0, 4), (1, 8))),
        "left_v": noise(arg_keys[1], (NT, K, B, R), 0.006, 0.035888672, ((0, 4), (1, 8))),
        "tile_p": noise(arg_keys[2], (NT, C, B, R), 1.0, 6.0, ((0, 4),)),
        "tile_q": noise(arg_keys[3], (NT, C, B, R), 0.09, 0.5390625, ((0, 4),)),
        "sketch": noise(arg_keys[4], (B, R), 1.0, 6.0),
        "tile_cols": set_ends(jax.random.randint(arg_keys[5], (NT, C), 0, NT), jax.random.fold_in(arg_keys[5], 1), 0, NT - 1).astype(jnp.int32),
    }


def from_gram(gram, sample):
    order = gram.shape[0]
    ridge = 1e-06 * jnp.trace(gram) / order
    gram = gram + ridge * jnp.eye(order, dtype=jnp.float32)
    triangle = jnp.linalg.cholesky(gram)
    return jax.scipy.linalg.solve_triangular(triangle, sample.T, lower=True).T

def reference(left_u, left_v, tile_p, tile_q, sketch, tile_cols):
    highest = lax.Precision.HIGHEST
    ntile, per_row = tile_cols.shape
    factor_scale = math.sqrt(B)
    omega_f = sketch.astype(jnp.float32)

    def one_tile(target):
        row_id = target // per_row
        slot = target % per_row
        column = tile_cols[row_id, slot]
        row_u = left_u[row_id].astype(jnp.float32)
        row_v = left_v[row_id].astype(jnp.float32)
        col_u = left_u[column].astype(jnp.float32)
        col_v = left_v[column].astype(jnp.float32)
        left_p = tile_p[row_id, slot].astype(jnp.float32)
        right_q = tile_q[row_id, slot].astype(jnp.float32)
        coupling = jnp.einsum('kbr,kbs->krs', row_v, col_v, precision=highest)
        sketched = jnp.einsum('kbs,bt->kst', col_u, omega_f, precision=highest)
        coupled = jnp.einsum('krs,kst->krt', coupling, sketched, precision=highest)
        coupled = coupled.astype(jnp.bfloat16).astype(jnp.float32)
        sample = jnp.dot(left_p, jnp.dot(right_q.T, omega_f, precision=highest), precision=highest)
        sample = sample - jnp.einsum('kbr,krt->bt', row_u, coupled, precision=highest)
        gram = jnp.dot(sample.T, sample, precision=highest)
        ortho_basis = from_gram(gram, sample)
        basis_half = ortho_basis.astype(jnp.bfloat16).astype(jnp.float32)
        inner_a = jnp.einsum('kbr,bt->krt', row_u, basis_half, precision=highest)
        inner_b = jnp.einsum('krs,krt->kst', coupling, inner_a, precision=highest)
        inner_b = inner_b.astype(jnp.bfloat16).astype(jnp.float32)
        new_right = jnp.dot(right_q, jnp.dot(left_p.T, ortho_basis, precision=highest), precision=highest)
        new_right = new_right - jnp.einsum('kbs,kst->bt', col_u, inner_b, precision=highest)
        return (ortho_basis * factor_scale, new_right / factor_scale)
    lefts, rights = lax.map(one_tile, jnp.arange(ntile * per_row, dtype=jnp.int32))
    shape = (ntile, per_row, lefts.shape[1], lefts.shape[2])
    return (lefts.reshape(shape), rights.reshape(shape))
```

```python
import functools
import math

import jax
import jax.numpy as jnp
from jax import lax
from jax.experimental import pallas as pl
from jax.experimental.pallas import tpu as pltpu
from jax.sharding import PartitionSpec as P


HIGHEST = lax.Precision.HIGHEST
F32 = jnp.float32
BF16 = jnp.bfloat16


def inverse_factor_kernel(gram_ref, out_ref, work_ref):
    count, order, _ = gram_ref.shape
    step = 16
    row = lax.broadcasted_iota(jnp.int32, (order, order), 0)
    lane = lax.broadcasted_iota(jnp.int32, (order, order), 1)
    eye = jnp.where(row == lane, 1.0, 0.0).astype(F32)
    for t in range(count):
        gram = gram_ref[t]
        ridge = 1e-06 * jnp.sum(gram * eye, keepdims=True) / order
        work_ref[t, :, :order] = gram + ridge * eye
        work_ref[t, :, order:] = eye
    below = lax.broadcasted_iota(jnp.int32, (step, 1), 0)
    for start in range(0, order, step):
        panels = [work_ref[t, start : start + step, :] for t in range(count)]
        pivots = [jnp.zeros((step, 1), F32) for _ in range(count)]
        for p in range(step):
            for t in range(count):
                panel = panels[t]
                column = panel[:, start + p : start + p + 1]
                pivot = column[p : p + 1, :]
                pivots[t] = jnp.where(below == p, pivot, pivots[t])
                factor = jnp.where(below > p, column / pivot, 0.0)
                panels[t] = panel - factor * panel[p : p + 1, :]
        for t in range(count):
            panel = panels[t]
            out_ref[t, start : start + step, :] = panel[:, order:] * lax.rsqrt(pivots[t])
            if start + step < order:
                scaled = panel[:, start + step : order] / pivots[t]
                update = lax.dot_general(
                    scaled, panel, (((0,), (0,)), ((), ())), precision=HIGHEST, preferred_element_type=F32
                )
                work_ref[t, start + step :, :] = work_ref[t, start + step :, :] - update


def inverse_factor(gram):
    count, order, _ = gram.shape
    return pl.pallas_call(
        inverse_factor_kernel,
        out_shape=jax.ShapeDtypeStruct((count, order, order), F32),
        scratch_shapes=[pltpu.VMEM((count, order, 2 * order), F32)],
    )(gram)


def body(left_u, left_v, tile_p, tile_q, sketch, tile_cols):
    rows = lax.axis_size("rows")
    me = lax.axis_index("rows")
    u, v, p, q = left_u[0], left_v[0], tile_p[0], tile_q[0]
    cols = tile_cols[0]
    panels, width, rank = u.shape
    tiles = cols.shape[0]
    factor_scale = math.sqrt(width)
    row_block = width // lax.axis_size("inner")
    offset = lax.axis_index("inner") * row_block

    planes = max(rows // 2, 1)
    first = (rows - planes) // 2
    part = panels // planes

    def to_planes(array):
        got = {0: lax.dynamic_slice_in_dim(array, (me - first) * part, part, 0)}
        for d in range(-(first + planes), first + planes + 1):
            pairs = [(s, s + d) for s in range(rows) if first <= s + d < first + planes]
            if d and pairs:
                piece = lax.dynamic_slice_in_dim(array, (me + d - first) * part, part, 0)
                got[d] = lax.ppermute(piece, "rows", pairs)
        return got

    def by_row(got):
        keys = sorted(got)
        out = []
        for j in range(rows):
            pick = jnp.zeros_like(got[0])
            for d in keys:
                pick = jnp.where(me - d == j, got[d], pick)
            out.append(pick)
        return jnp.stack(out)

    def to_rows(array):
        got = {0: lax.dynamic_index_in_dim(array, me, 0, keepdims=False)}
        for d in range(-(first + planes), first + planes + 1):
            pairs = [(g, g + d) for g in range(first, first + planes) if 0 <= g + d < rows]
            if d and pairs:
                piece = lax.dynamic_index_in_dim(array, me + d, 0, keepdims=False)
                got[d] = lax.ppermute(piece, "rows", pairs)
        out = []
        for g in range(planes):
            pick = jnp.zeros_like(got[0])
            for d in sorted(got):
                pick = jnp.where(me - d == first + g, got[d], pick)
            out.append(pick)
        return jnp.concatenate(out, axis=1)

    sketched = jnp.einsum("kbs,bt->kst", u, sketch, preferred_element_type=F32)
    got_v = to_planes(v)
    got_s = to_planes(sketched)
    u_late, got_v = lax.optimization_barrier((u, got_v))
    all_v = by_row(got_v)
    all_s = by_row(got_s)

    ups, downs = [], []
    up = down = u_late
    for d in range(1, rows):
        up = lax.ppermute(up, "rows", [(s, s + 1) for s in range(d - 1, rows - 1)])
        down = lax.ppermute(down, "rows", [(s, s - 1) for s in range(1, rows - d + 1)])
        ups.append(up)
        downs.append(down)

    coupling = jnp.einsum("ikbr,jkbs->ijkrs", all_v, all_v, preferred_element_type=F32)
    coupled = jnp.einsum("ijkrs,jkst->ijkrt", coupling, all_s, precision=HIGHEST).astype(BF16)
    coupled = to_rows(coupled)
    coupling = to_rows(coupling)
    samples = jnp.einsum("kbr,jkrt->jbt", u, coupled, preferred_element_type=F32)
    sample_sum = lax.psum(samples, "inner")
    sketched_q = jnp.einsum("nbr,bt->nrt", q, sketch, preferred_element_type=F32)
    pf = p.astype(F32)
    tile_sample = jnp.einsum("nbr,nrt->nbt", pf, sketched_q, precision=HIGHEST)
    sample = tile_sample - sample_sum[cols]
    gram = jnp.einsum("nbr,nbs->nrs", sample, sample, precision=HIGHEST)
    inverse = inverse_factor(gram)
    basis = jnp.einsum("nbr,nsr->nbs", sample, inverse, precision=HIGHEST)
    basis_rows = lax.dynamic_slice_in_dim(basis, offset, row_block, 1)
    basis_half = basis.astype(BF16)
    inner_a = jnp.einsum("kbr,nbt->nkrt", u, basis_half, preferred_element_type=F32)
    inner_b = jnp.einsum("nkrs,nkrt->nkst", coupling[cols], inner_a, precision=HIGHEST).astype(BF16)

    all_u = []
    for j in range(rows):
        pick = u
        for d in range(1, rows):
            pick = jnp.where(me - d == j, ups[d - 1], pick)
            pick = jnp.where(me + d == j, downs[d - 1], pick)
        all_u.append(pick)
    all_u = jnp.stack(all_u)

    def one_right(n):
        return jnp.einsum("kbs,kst->bt", all_u[cols[n]], inner_b[n], preferred_element_type=F32)

    rights = lax.map(one_right, jnp.arange(tiles, dtype=jnp.int32))
    projected = lax.psum_scatter(rights, "inner", scatter_dimension=1, tiled=True)
    p_basis = jnp.einsum("nbr,nbt->nrt", pf, basis, precision=HIGHEST)
    q_rows = lax.dynamic_slice_in_dim(q, offset, row_block, 1).astype(F32)
    new_right = jnp.einsum("nbr,nrt->nbt", q_rows, p_basis, precision=HIGHEST) - projected
    return ((basis_rows * factor_scale)[None], (new_right / factor_scale)[None])


def solution(mesh):
    return jax.shard_map(
        body,
        mesh=mesh,
        in_specs=(
            P("rows", "inner", None, None),
            P("rows", "inner", None, None),
            P("rows", None, None, None),
            P("rows", None, None, None),
            P(),
            P("rows", None),
        ),
        out_specs=(P("rows", None, "inner", None), P("rows", None, "inner", None)),
        check_vma=False,
    )
```

```python
import math

import jax
import jax.numpy as jnp
from jax import lax
from jax.experimental import pallas as pl
from jax.experimental.pallas import tpu as pltpu
from jax.sharding import PartitionSpec as P


HIGHEST = lax.Precision.HIGHEST
F32 = jnp.float32
BF16 = jnp.bfloat16
I16 = jnp.int16
I32 = jnp.int32
EXTRA = 16


def full_spec(shape):
    return pl.BlockSpec(shape, lambda *_: (0,) * len(shape))


def contract(a, b, da, db):
    return lax.dot_general(a, b, (((da,), (db,)), ((), ())), preferred_element_type=F32)


def split(x):
    high = x.astype(BF16)
    return high, (x - high.astype(F32)).astype(BF16)


def split_rhs(x):
    high, low = split(x)
    return jnp.concatenate(
        [jnp.concatenate([high, low], 1), jnp.concatenate([high, jnp.zeros_like(low)], 1)], 0
    )


def split_dot(x, rhs):
    half = rhs.shape[1] // 2
    both = contract(jnp.concatenate(split(x), 1), rhs, 1, 0)
    return both[:, :half] + both[:, half:]


def encode(x):
    top = jnp.maximum(jnp.max(jnp.abs(x), axis=0, keepdims=True), 2.0**-100)
    exponent = jnp.floor(jnp.log2(top))
    value = jnp.floor(x * jnp.exp2(13.0 - exponent) + 0.5).astype(I32).astype(I16)
    return value, jnp.broadcast_to(exponent.astype(I32), (EXTRA, x.shape[1])).astype(I16)


def decode(ref, index, block):
    exponent = ref[index, block:, :].astype(I32)[:1].astype(F32)
    return ref[index, :block, :].astype(I32).astype(F32) * jnp.exp2(exponent - 13.0)


def early_kernel(u_ref, sketch_ref, ut_ref, sketched_ref):
    flipped = u_ref[0].T
    ut_ref[0] = flipped
    sketched_ref[0] = contract(flipped, sketch_ref[...], 1, 0)


def early(u, sketch):
    panels, width, rank = u.shape
    return pl.pallas_call(
        early_kernel,
        grid=(panels,),
        in_specs=[pl.BlockSpec((1, width, rank), lambda k: (k, 0, 0)), full_spec(sketch.shape)],
        out_specs=[
            pl.BlockSpec((1, rank, width), lambda k: (k, 0, 0)),
            pl.BlockSpec((1, rank, rank), lambda k: (k, 0, 0)),
        ],
        out_shape=[
            jax.ShapeDtypeStruct((panels, rank, width), BF16),
            jax.ShapeDtypeStruct((panels, rank, rank), F32),
        ],
        name="early",
    )(u, sketch)


def first_term_kernel(p_ref, q_ref, sketch_ref, out_ref):
    rank = p_ref.shape[2]
    middle = contract(q_ref[0], sketch_ref[...], 0, 0)
    both = contract(p_ref[0], jnp.concatenate(split(middle), 1), 1, 0)
    out_ref[0] = both[:, :rank] + both[:, rank:]


def first_term(p, q, sketch):
    tiles, width, rank = p.shape
    spec = pl.BlockSpec((1, width, rank), lambda c: (c, 0, 0))
    return pl.pallas_call(
        first_term_kernel,
        grid=(tiles,),
        in_specs=[spec, spec, full_spec(sketch.shape)],
        out_specs=spec,
        out_shape=jax.ShapeDtypeStruct((tiles, width, rank), F32),
        name="first_term",
    )(p, q, sketch)


def couple(me, got_v, got_s, layout):
    rows, first, planes, part = layout
    keys = sorted(got_v)
    width, rank = got_v[0].shape[1:]
    shifts = row_shifts(layout)

    def kernel(me_ref, *refs):
        v_in, refs = refs[: len(keys)], refs[len(keys) :]
        s_in, refs = refs[: len(keys)], refs[len(keys) :]
        coupled_out, refs = refs[: len(shifts)], refs[len(shifts) :]
        coupling_out, refs = refs[: len(shifts)], refs[len(shifts) :]
        v_all, s_all, coupled_all, coupling_all, sems = refs
        here = me_ref[0]

        def copies(g):
            out = []
            for at, d in enumerate(keys):
                j = g - d
                if 0 <= j < rows:
                    out.append(pltpu.make_async_copy(v_in[at], v_all.at[j], sems.at[j]))
                    out.append(pltpu.make_async_copy(s_in[at], s_all.at[j], sems.at[rows + j]))
            return out

        for g in range(first, first + planes):

            @pl.when(here == g)
            def _():
                for copy in copies(g):
                    copy.start()
                for copy in copies(g):
                    copy.wait()

        @pl.when((here >= first) & (here < first + planes))
        def _():
            for k in range(part):
                wide = jnp.concatenate([v_all[j, k] for j in range(rows)], 1)
                gram = contract(wide, wide, 0, 0)
                for j in range(rows):
                    column = gram[:, j * rank : (j + 1) * rank]
                    product = split_dot(column, split_rhs(s_all[j, k])).astype(BF16)
                    for i in range(rows):
                        coupled_all[i, j, k] = product[i * rank : (i + 1) * rank]
                        coupling_all[j, i, k] = column[i * rank : (i + 1) * rank]
            for at, d in enumerate(shifts):
                target = jnp.clip(here + d, 0, rows - 1)
                coupled_out[at][...] = coupled_all[target]
                coupling_out[at][...] = coupling_all[target]

    any_spec = pl.BlockSpec(memory_space=pl.ANY)
    small = (rows, part, rank, rank)
    out = pl.pallas_call(
        kernel,
        in_specs=[pl.BlockSpec(memory_space=pltpu.SMEM)] + [any_spec] * (2 * len(keys)),
        out_specs=[full_spec(small)] * (2 * len(shifts)),
        grid=(1,),
        out_shape=[jax.ShapeDtypeStruct(small, BF16)] * len(shifts)
        + [jax.ShapeDtypeStruct(small, F32)] * len(shifts),
        scratch_shapes=[
            pltpu.VMEM((rows, part, width, rank), BF16),
            pltpu.VMEM((rows, part, rank, rank), F32),
            pltpu.VMEM((rows,) + small, BF16),
            pltpu.VMEM((rows,) + small, F32),
            pltpu.SemaphoreType.DMA((2 * rows,)),
        ],
        name="couple",
    )(me[None], *[got_v[d] for d in keys], *[got_s[d] for d in keys])
    return dict(zip(shifts, out[: len(shifts)])), dict(zip(shifts, out[len(shifts) :]))


def row_shifts(layout):
    rows, first, planes, _ = layout
    return [d for d in range(-(first + planes) + 1, rows - first) if any(0 <= g + d < rows for g in range(first, first + planes))]


def at_slice(here, d, layout, action):
    rows, first, planes, _ = layout
    for g in range(planes):
        if 0 <= first + g + d < rows:
            pl.when(here - d == first + g)(lambda g=g: action(g))


def partial_samples(scalars, u, got, layout, chips):
    rows, _, _, part = layout
    keys = sorted(got)
    panels, width, rank = u.shape
    block = width // (2 * chips)

    def kernel(s_ref, u_ref, *refs):
        pieces, out_ref, rhs = refs[: len(keys)], refs[-2], refs[-1]

        @pl.when(pl.program_id(0) == 0)
        def _():
            for at, d in enumerate(keys):

                def fill(g, at=at):
                    for k in range(part):
                        for j in range(rows):
                            low = (g * part + k) * rank
                            rhs[low : low + rank, j * rank : (j + 1) * rank] = pieces[at][j, k]

                at_slice(s_ref[0], d, layout, fill)

        wide = jnp.concatenate([u_ref[k] for k in range(panels)], 1)
        out = contract(wide, rhs[...], 1, 0)
        for j in range(rows):
            out_ref[j, 0] = out[:, j * rank : (j + 1) * rank]

    small = (rows, part, rank, rank)
    return pl.pallas_call(
        kernel,
        grid_spec=pltpu.PrefetchScalarGridSpec(
            num_scalar_prefetch=1,
            grid=(chips,),
            in_specs=[pl.BlockSpec((panels, block, rank), lambda i, s: (0, 2 * i + s[1], 0))]
            + [full_spec(small)] * len(keys),
            out_specs=pl.BlockSpec((rows, 1, block, rank), lambda i, s: (0, i, 0, 0)),
            scratch_shapes=[pltpu.VMEM((panels * rank, rows * rank), BF16)],
        ),
        out_shape=jax.ShapeDtypeStruct((rows, chips, block, rank), F32),
        name="partial_samples",
    )(scalars, u, *[got[d] for d in keys])


def encode_for_chips(chip, mine, other):
    count, chips, block, rank = mine.shape

    def kernel(s_ref, mine_ref, other_ref, *outs):
        for d in range(chips):

            @pl.when(pl.program_id(0) == d)
            def _(d=d):
                for n in range(count):
                    value, exponent = encode(mine_ref[n, 0] + other_ref[n, 0])
                    outs[d][n, :block, :] = value
                    outs[d][n, block:, :] = exponent

    spec = pl.BlockSpec((count, 1, block, rank), lambda d, s: (0, (s[0] + d) % chips, 0, 0))
    coded = (count, block + EXTRA, rank)
    return pl.pallas_call(
        kernel,
        grid_spec=pltpu.PrefetchScalarGridSpec(
            num_scalar_prefetch=1,
            grid=(chips,),
            in_specs=[spec, spec],
            out_specs=[full_spec(coded)] * chips,
        ),
        out_shape=[jax.ShapeDtypeStruct(coded, I16)] * chips,
        name="encode_for_chips",
    )(chip[None], mine, other)


def add_coded(parts):
    count, tall, rank = parts[0].shape
    block = tall - EXTRA

    def kernel(*refs):
        total = decode(refs[0], 0, block)
        for ref in refs[1:-1]:
            total = total + decode(ref, 0, block)
        value, exponent = encode(total)
        refs[-1][0, :block, :] = value
        refs[-1][0, block:, :] = exponent

    spec = pl.BlockSpec((1, tall, rank), lambda n: (n, 0, 0))
    return pl.pallas_call(
        kernel,
        grid=(count,),
        in_specs=[spec] * len(parts),
        out_specs=spec,
        out_shape=jax.ShapeDtypeStruct(parts[0].shape, I16),
        name="add_coded",
    )(*parts)


def inverse_factors(gram_ref, work_ref, out_ref):
    count, order, _ = gram_ref.shape
    step = 16
    row = lax.broadcasted_iota(I32, (order, order), 0)
    lane = lax.broadcasted_iota(I32, (order, order), 1)
    eye = jnp.where(row == lane, 1.0, 0.0).astype(F32)
    for t in range(count):
        gram = gram_ref[t]
        ridge = 1e-06 * jnp.sum(gram * eye, keepdims=True) / order
        work_ref[t, :, :order] = gram + ridge * eye
        work_ref[t, :, order:] = eye
    below = lax.broadcasted_iota(I32, (step, 1), 0)
    for start in range(0, order, step):
        panels = [work_ref[t, start : start + step, :] for t in range(count)]
        pivots = [jnp.zeros((step, 1), F32) for _ in range(count)]
        for p in range(step):
            for t in range(count):
                panel = panels[t]
                column = panel[:, start + p : start + p + 1]
                pivot = column[p : p + 1, :]
                pivots[t] = jnp.where(below == p, pivot, pivots[t])
                factor = jnp.where(below > p, column / pivot, 0.0)
                panels[t] = panel - factor * panel[p : p + 1, :]
        for t in range(count):
            panel = panels[t]
            out_ref[t, start : start + step, :] = panel[:, order:] * lax.rsqrt(pivots[t])
            if start + step < order:
                scaled = panel[:, start + step : order] / pivots[t]
                update = lax.dot_general(
                    scaled, panel, (((0,), (0,)), ((), ())), precision=HIGHEST, preferred_element_type=F32
                )
                work_ref[t, start + step :, :] = work_ref[t, start + step :, :] - update


def orthogonalize(scalars, term, p, blocks, chips):
    tiles, width, rank = p.shape
    block = width // (2 * chips)
    scale = math.sqrt(width)
    flat = [blocks[d][h] for d in range(chips) for h in range(2)]

    def kernel(s_ref, term_ref, p_ref, *refs):
        coded, refs = refs[: len(flat)], refs[len(flat) :]
        half_ref, left_ref, pb_ref, sample, gram, work, inverse = refs
        at = pl.program_id(0)
        tile = at % tiles
        chip, core = s_ref[0], s_ref[1]

        @pl.when(at < tiles)
        def _():
            total = jnp.zeros((rank, 2 * rank), F32)
            for d in range(chips):
                for h in range(2):
                    start = (2 * ((chip + chips - d) % chips) + (core + h) % 2) * block
                    start = pl.multiple_of(start, block)
                    x = term_ref[0, pl.ds(start, block), :] - decode(coded[2 * d + h], s_ref[2 + tile], block)
                    sample[tile, pl.ds(start, block), :] = x
                    high, low = split(x)
                    total = total + contract(high, jnp.concatenate([high, low], 1), 0, 0)
            cross = total[:, rank:]
            gram[tile] = total[:, :rank] + cross + cross.T

        @pl.when(at == tiles - 1)
        def _():
            inverse_factors(gram, work, inverse)

        @pl.when(at >= tiles)
        def _():
            basis = split_dot(sample[tile], split_rhs(inverse[tile].T))
            sample[tile] = basis
            high, low = split(basis)
            half_ref[0] = high
            both = contract(p_ref[0], jnp.concatenate([high, low], 1), 0, 0)
            pb_ref[0] = both[:, :rank] + both[:, rank:]
            start = pl.multiple_of((2 * chip + core) * block, block)
            left_ref[0] = sample[tile, pl.ds(start, block), :] * scale

    second = lambda i: jnp.maximum(i - tiles, 0)
    coded_shape = flat[0].shape
    return pl.pallas_call(
        kernel,
        grid_spec=pltpu.PrefetchScalarGridSpec(
            num_scalar_prefetch=1,
            grid=(2 * tiles,),
            in_specs=[
                pl.BlockSpec((1, width, rank), lambda i, s: (jnp.minimum(i, tiles - 1), 0, 0)),
                pl.BlockSpec((1, width, rank), lambda i, s: (second(i), 0, 0)),
            ]
            + [full_spec(coded_shape)] * len(flat),
            out_specs=[
                pl.BlockSpec((1, width, rank), lambda i, s: (second(i), 0, 0)),
                pl.BlockSpec((1, block, rank), lambda i, s: (second(i), 0, 0)),
                pl.BlockSpec((1, rank, rank), lambda i, s: (second(i), 0, 0)),
            ],
            scratch_shapes=[
                pltpu.VMEM((tiles, width, rank), F32),
                pltpu.VMEM((tiles, rank, rank), F32),
                pltpu.VMEM((tiles, rank, 2 * rank), F32),
                pltpu.VMEM((tiles, rank, rank), F32),
            ],
        ),
        out_shape=[
            jax.ShapeDtypeStruct((tiles, width, rank), BF16),
            jax.ShapeDtypeStruct((tiles, block, rank), F32),
            jax.ShapeDtypeStruct((tiles, rank, rank), F32),
        ],
        name="orthogonalize",
    )(scalars, term, p, *flat)


def project(scalars, ut, half, got, layout):
    rows, _, _, part = layout
    keys = sorted(got)
    tiles, width, rank = half.shape
    deep = ut.shape[0]
    group = 2 if tiles % 2 == 0 else 1

    def kernel(s_ref, ut_ref, half_ref, *refs):
        pieces, out_ref, coupling = refs[: len(keys)], refs[-2], refs[-1]

        @pl.when(pl.program_id(0) == 0)
        def _():
            for at, d in enumerate(keys):

                def fill(g, at=at):
                    for k in range(part):
                        coupling[:, g * part + k] = pieces[at][:, k]

                at_slice(s_ref[0], d, layout, fill)

        wide = jnp.concatenate([half_ref[t] for t in range(group)], 1)
        inner_a = contract(ut_ref[...], wide, 1, 0)
        for t in range(group):
            column = s_ref[1 + pl.program_id(0) * group + t]
            for k in range(deep // rank):
                part_a = inner_a[k * rank : (k + 1) * rank, t * rank : (t + 1) * rank]
                inner_b = split_dot(coupling[column, k], split_rhs(part_a))
                out_ref[t, k * rank : (k + 1) * rank, :] = inner_b.astype(BF16)

    small = (rows, part, rank, rank)
    return pl.pallas_call(
        kernel,
        grid_spec=pltpu.PrefetchScalarGridSpec(
            num_scalar_prefetch=1,
            grid=(tiles // group,),
            in_specs=[full_spec(ut.shape), pl.BlockSpec((group, width, rank), lambda i, s: (i, 0, 0))]
            + [full_spec(small)] * len(keys),
            out_specs=pl.BlockSpec((group, deep, rank), lambda i, s: (i, 0, 0)),
            scratch_shapes=[pltpu.VMEM((rows, deep // rank, rank, rank), F32)],
        ),
        out_shape=jax.ShapeDtypeStruct((tiles, deep, rank), BF16),
        name="project",
    )(scalars, ut, half, *[got[d] for d in keys])


def partial_rights(scalars, u, buffers, inner_b, rows, chips):
    panels, width, rank = u.shape
    tiles = inner_b.shape[0]
    block = width // (2 * chips)

    def kernel(s_ref, inner_ref, *refs):
        sources, out_ref, chosen = refs[:-2], refs[-2], refs[-1]
        for j in range(rows):
            for at, source in enumerate(sources):

                @pl.when(s_ref[1 + j] == at)
                def _(j=j, source=source):
                    for k in range(panels):
                        chosen[j, :, k * rank : (k + 1) * rank] = source[k]

        for t in range(tiles):
            out_ref[t, 0] = contract(chosen[s_ref[1 + rows + t]], inner_ref[t], 1, 0)

    piece = (panels, block, rank)
    return pl.pallas_call(
        kernel,
        grid_spec=pltpu.PrefetchScalarGridSpec(
            num_scalar_prefetch=1,
            grid=(chips,),
            in_specs=[full_spec(inner_b.shape), pl.BlockSpec(piece, lambda i, s: (0, 2 * i + s[0], 0))]
            + [pl.BlockSpec(piece, lambda i, s: (0, i, 0))] * len(buffers),
            out_specs=pl.BlockSpec((tiles, 1, block, rank), lambda i, s: (0, i, 0, 0)),
            scratch_shapes=[pltpu.VMEM((rows, block, panels * rank), BF16)],
        ),
        out_shape=jax.ShapeDtypeStruct((tiles, chips, block, rank), F32),
        name="partial_rights",
    )(scalars, inner_b, u, *buffers)


def finish(own, q, p_basis, coded):
    tiles, tall, rank = coded[0].shape
    block = tall - EXTRA
    scale = math.sqrt(q.shape[1])

    def kernel(s_ref, q_ref, pb_ref, *refs):
        total = decode(refs[0], 0, block)
        for ref in refs[1:-1]:
            total = total + decode(ref, 0, block)
        both = contract(q_ref[0], jnp.concatenate(split(pb_ref[0]), 1), 1, 0)
        refs[-1][0] = (both[:, :rank] + both[:, rank:] - total) * (1.0 / scale)

    spec = pl.BlockSpec((1, tall, rank), lambda c, s: (c, 0, 0))
    return pl.pallas_call(
        kernel,
        grid_spec=pltpu.PrefetchScalarGridSpec(
            num_scalar_prefetch=1,
            grid=(tiles,),
            in_specs=[
                pl.BlockSpec((1, block, rank), lambda c, s: (c, s[0], 0)),
                pl.BlockSpec((1, rank, rank), lambda c, s: (c, 0, 0)),
            ]
            + [spec] * len(coded),
            out_specs=pl.BlockSpec((1, block, rank), lambda c, s: (c, 0, 0)),
        ),
        out_shape=jax.ShapeDtypeStruct((tiles, block, rank), F32),
        name="finish",
    )(own[None], q, p_basis, *coded)


def body(left_u, left_v, tile_p, tile_q, sketch, tile_cols):
    rows = lax.axis_size("rows")
    inner = lax.axis_size("inner")
    me = lax.axis_index("rows").astype(I32)
    own = lax.axis_index("inner").astype(I32)
    chips = inner // 2
    chip, core = own // 2, own % 2
    u, v, p, q = left_u[0], left_v[0], tile_p[0], tile_q[0]
    cols = tile_cols[0]
    panels, width, rank = u.shape
    block = width // inner

    planes = max(rows // 2, 1)
    first = (rows - planes) // 2
    part = panels // planes
    layout = (rows, first, planes, part)

    def to_planes(array):
        got = {0: lax.dynamic_slice_in_dim(array, (me - first) * part, part, 0)}
        for d in sorted(range(-rows + 1, rows), key=lambda d: -abs(d)):
            pairs = [(s, s + d) for s in range(rows) if first <= s + d < first + planes]
            if d and pairs:
                piece = lax.dynamic_slice_in_dim(array, (me + d - first) * part, part, 0)
                got[d] = lax.ppermute(piece, "rows", pairs)
        return got

    def to_rows(pieces):
        got = {}
        for d, piece in pieces.items():
            pairs = [(g, g + d) for g in range(first, first + planes) if 0 <= g + d < rows]
            got[d] = lax.ppermute(piece, "rows", pairs) if d else piece
        return got

    swap = [(m, m ^ 1) for m in range(inner)]
    turn = [[(m, (m + 2 * d) % inner) for m in range(inner)] for d in range(chips)]

    got_v = to_planes(v)
    ut, sketched = early(u, sketch)
    got_s = to_planes(sketched)
    term = first_term(p, q, sketch)

    by_block = u.reshape(panels, chips, 2, block, rank)
    parities = [1 - core, core]
    chunks = [
        lax.dynamic_index_in_dim(by_block, parity, 2, keepdims=False).reshape(panels, chips * block, rank)
        for parity in parities
    ]
    outward = [(s, s + 1) for s in range(rows // 2, rows - 1)] + [(s, s - 1) for s in range(1, rows // 2)]
    upward = [(s, s + 1) for s in range(rows // 2)]
    downward = [(s, s - 1) for s in range(rows // 2, rows)]
    outer = [lax.ppermute(chunk, "rows", outward) for chunk in chunks]
    late, got_v = lax.optimization_barrier((chunks, got_v))
    ups = [[lax.ppermute(chunk, "rows", upward)] for chunk in late]
    downs = [[lax.ppermute(chunk, "rows", downward)] for chunk in late]

    coupled, coupling = couple(me, got_v, got_s, layout)
    coupled = to_rows(coupled)
    coupling = to_rows(coupling)

    send = partial_samples(jnp.stack([me, 1 - core]), u, coupled, layout, chips)
    received = lax.ppermute(send, "inner", swap)
    mine = partial_samples(jnp.stack([me, core]), u, coupled, layout, chips)
    coded = encode_for_chips(chip, mine, received)
    coded = add_coded([coded[0]] + [lax.ppermute(coded[d], "inner", turn[d]) for d in range(1, chips)])
    same = [coded] + [lax.ppermute(coded, "inner", turn[d]) for d in range(1, chips)]
    blocks = [(x, lax.ppermute(x, "inner", swap)) for x in same]

    for d in range(2, rows):
        for c in range(2):
            up, down = ups[c][-1], downs[c][-1]
            if d == 2:
                if any(s in [b for _, b in outward] for s in range(1, rows - 1)):
                    up = jnp.where(me > rows // 2, outer[c], up)
                    down = jnp.where(me < rows // 2 - 1, outer[c], down)
            ups[c].append(lax.ppermute(up, "rows", [(s, s + 1) for s in range(d - 1, rows - 1)]))
            downs[c].append(lax.ppermute(down, "rows", [(s, s - 1) for s in range(1, rows - d + 1)]))
    buffers = [[outer[c]] + ups[c] + downs[c] for c in range(2)]

    def source_of(i, j):
        if i == j:
            return 0
        d = abs(i - j)
        if d == 1 and (j, i) in outward:
            return 1
        return 1 + d if j < i else rows + d

    table = jnp.array([[source_of(i, j) for j in range(rows)] for i in range(rows)], I32)
    sources = lax.dynamic_index_in_dim(table, me, 0, keepdims=False)

    half, new_left, p_basis = orthogonalize(
        jnp.concatenate([jnp.stack([chip, core]), cols]), term, p, blocks, chips
    )
    inner_b = project(
        jnp.concatenate([me[None], cols]), ut.reshape(panels * rank, width), half, coupling, layout
    )
    rights = [
        partial_rights(
            jnp.concatenate([parities[c][None], sources, cols]), u, buffers[c], inner_b, rows, chips
        )
        for c in range(2)
    ]
    received = lax.ppermute(rights[0], "inner", swap)
    coded = encode_for_chips(chip, rights[1], received)
    coded = [coded[0]] + [lax.ppermute(coded[d], "inner", turn[d]) for d in range(1, chips)]
    new_right = finish(own, q, p_basis, coded)
    return new_left[None], new_right[None]


def solution(mesh):
    return jax.shard_map(
        body,
        mesh=mesh,
        in_specs=(
            P("rows", "inner", None, None),
            P("rows", "inner", None, None),
            P("rows", None, None, None),
            P("rows", None, None, None),
            P(),
            P("rows", None),
        ),
        out_specs=(P("rows", None, "inner", None), P("rows", None, "inner", None)),
        check_vma=False,
    )
```
